32 devices in a mesh: groups: 2 (over x), seq: 16 (over z, y, core).
Axes of the slice: x: 2, y: 2, z: 4, core: 2. Of those that a mesh axis runs over, the one named last changes fastest.
Arguments:
- queries: bfloat16 [4096, 8192], P(('groups', 'seq')), parts along dimension 0, may hold values from -4.5 to 4.5
- keyvalue: bfloat16 [4096, 2048], P(('groups', 'seq')), parts along dimension 0, may hold values from -4.5 to 4.5
- doc_ids: int32 [4096], P(('groups', 'seq')), parts along dimension 0, may hold values from 0 to 7, never falling along the last dimension, each value on 1 to 512 neighbouring positions
- owner_tiles: int32 [32, 2], P(('groups', 'seq')), parts along dimension 0, may hold values from 0 to 15, as said below
- tile_counts: int32 [32], P(('groups', 'seq')), parts along dimension 0, may hold values from 0 to 2, as said below
Outputs:
- owned: bfloat16 [8192, 8192], P(('groups', 'seq')), parts along dimension 0
The draws below stay inside these ranges and needn't reach their ends.
There are 2 independent parts, one for each index of `groups`. The reference program is written for one: setup_inputs(seed, part) draws one part's arguments, and reference() takes and returns one part's arrays. A program takes and returns all parts, laid end to end along the dimension named above; each array names one. Nothing has to cross between parts.
Inputs may be any that keep to these rules, and one draw needn't show every extreme that they name: `owner_tiles`: over the slots below each owner's count, every tile 0 to 15 is listed exactly once; the other slots hold 0. Tile t is listed either by its holder, the owner o with o * 128 <= t * 128 < (o + 1) * 128, or by the holder's partner, the owner whose index differs from the holder's by half the number of owners. `tile_counts`: the counts sum to 16; each is 0, 1 or 2, some owner has 2, and an owner has 2 exactly when its partner has 0.
All inputs are finite; a program needn't handle non-finite values.
Results may differ from the reference program's by a relative error of at most 0.0034.
Values may be sent and summed in bfloat16 or wider, within the bound.
A program may use at most 64 MiB of HBM per device.

```python
import math
import jax
import jax.numpy as jnp
import numpy as np
from jax import lax

QUERY_HEADS = 64
KEY_VALUE_HEADS = 8
HEAD_WIDTH = 128
TILE = 128
DOCUMENT_LIMIT = 512
TOK_DEV = 128
SLAB_TOKENS = 2048
NTILE = 16
CAP = 2
DOCS = 8
N_SEQ = 16


def draw_queries(key, part):
    owner_key = jax.random.fold_in(key, 11)
    value_rows = jax.random.truncated_normal(owner_key, -4.0, 4.0, (SLAB_TOKENS, QUERY_HEADS, HEAD_WIDTH))
    return value_rows.astype(jnp.float32).reshape(SLAB_TOKENS, QUERY_HEADS * HEAD_WIDTH).astype(jnp.bfloat16)


def draw_keyvalue(key, part):
    owner_key = jax.random.fold_in(key, 23)
    value_rows = jax.random.truncated_normal(owner_key, -4.0, 4.0, (SLAB_TOKENS, KEY_VALUE_HEADS, 2, HEAD_WIDTH))
    return value_rows.astype(jnp.float32).reshape(SLAB_TOKENS, KEY_VALUE_HEADS * 2 * HEAD_WIDTH).astype(jnp.bfloat16)


def owner_plan(key):
    base = jax.random.fold_in(key, 5113)
    leading_entry, second, third, fourth = jax.random.split(base, 4)
    half = N_SEQ // 2
    per_device = TOK_DEV // TILE
    pair_rank = jnp.argsort(jax.random.permutation(leading_entry, half))
    movers = jax.random.randint(second, (), 1, half // 2 + 1)
    moving = pair_rank < movers
    side = jax.random.randint(third, (half,), 0, 2)
    devices = jnp.arange(N_SEQ, dtype=jnp.int32)
    pair = devices % half
    lower = devices < half
    moving_dev = moving[pair]
    giver = moving_dev & ((side[pair] == 0) == lower)
    taker = moving_dev & jnp.logical_not(giver)
    counts = jnp.where(giver, 0, jnp.where(taker, CAP, per_device)).astype(jnp.int32)
    local_tiles = jnp.arange(per_device, dtype=jnp.int32)
    own = devices[:, None] * per_device + local_tiles[None, :]
    partner = (devices + half) % N_SEQ
    theirs = partner[:, None] * per_device + local_tiles[None, :]
    candidates = jnp.concatenate([own, jnp.where(taker[:, None], theirs, 0)], axis=1)
    candidates = jnp.where(giver[:, None], 0, candidates)
    slots = jnp.arange(CAP, dtype=jnp.int32)
    shuffled = jax.random.permutation(fourth, jnp.tile(slots[None, :], (N_SEQ, 1)), axis=1, independent=True)
    scores = shuffled + jnp.where(slots[None, :] < counts[:, None], 0, CAP)
    order = jnp.argsort(scores, axis=1, stable=True)
    lists = jnp.take_along_axis(candidates, order, axis=1)
    lists = jnp.where(slots[None, :] < counts[:, None], lists, 0).astype(jnp.int32)
    return (lists, counts)


def draw_owner_tiles(key, part):
    lists, counts = owner_plan(key)
    return lists


def draw_tile_counts(key, part):
    lists, counts = owner_plan(key)
    return counts


def length_profile(count, total, most, lean):
    portions = [(1 << 20) // math.isqrt(standing ** lean) + 1 for standing in range(2, count + 1)]
    surplus, given = total - most - (count - 1), [1] * (count - 1)
    while surplus > 0:
        free = [i for i in range(count - 1) if given[i] < most]
        whole, left = sum([portions[i] for i in free]), surplus
        for i in free:
            addition = min(most - given[i], max(1, left * portions[i] // whole), surplus)
            given[i] = given[i] + addition
            surplus = surplus - addition
    return np.array([most] + given)


def ragged_sizes(key, number_of, total, most, slope):
    if number_of == 2:
        one = jax.random.randint(key, (), max(1, total - most), min(most, total - 1) + 1)
        return jnp.stack([one, total - one])
    lengths = jnp.asarray(length_profile(number_of, total, most, slope), jnp.int32)
    twos = (number_of - 1) // 2
    donor, taker = lengths[1:1 + 2 * twos:2], lengths[2:2 + 2 * twos:2]
    margin = jnp.minimum(donor - 1, most - taker)
    shifted = jax.random.randint(jax.random.fold_in(key, 1), (twos,), 0, 1 << 20) % (margin + 1)
    lengths = lengths.at[1:1 + 2 * twos:2].set(donor - shifted).at[2:2 + 2 * twos:2].set(taker + shifted)
    return lengths[jax.random.permutation(jax.random.fold_in(key, 2), number_of)]


def setup_inputs(seed: int = 0, part: int = 0) -> dict:
    arg_keys = jax.random.split(jax.random.key(seed), 6)
    part_splits = jax.random.split(jax.random.fold_in(arg_keys[5], part), 6)
    return {
        "queries": draw_queries(jax.random.fold_in(jax.random.fold_in(arg_keys[5], part), 71), part),
        "keyvalue": draw_keyvalue(jax.random.fold_in(jax.random.fold_in(arg_keys[5], part), 71), part),
        "doc_ids": jnp.searchsorted(jnp.cumsum(ragged_sizes(part_splits[2], DOCS, SLAB_TOKENS, DOCUMENT_LIMIT, 2)), jnp.arange(SLAB_TOKENS), side="right").astype(jnp.int32),
        "owner_tiles": draw_owner_tiles(jax.random.fold_in(jax.random.fold_in(arg_keys[5], part), 71), part),
        "tile_counts": draw_tile_counts(jax.random.fold_in(jax.random.fold_in(arg_keys[5], part), 71), part),
    }


def attend(queries, keys, value_rows, allowed):
    scale = HEAD_WIDTH ** -0.5
    scores = jnp.einsum("rhgd,khd->hgrk", queries.astype(jnp.float32), keys.astype(jnp.float32)) * scale
    scores = jnp.where(allowed[None, None], scores, -jnp.inf)
    row_top = jnp.max(scores, axis=3, keepdims=True)
    exponent = jnp.exp(scores - row_top)
    totals = jnp.sum(exponent, axis=3, keepdims=True)
    weights = exponent.astype(jnp.bfloat16)
    mixed_rows = jnp.einsum("hgrk,khd->rhgd", weights.astype(jnp.float32), value_rows.astype(jnp.float32))
    return (mixed_rows / jnp.transpose(totals, (2, 0, 1, 3))).astype(jnp.bfloat16)


def reference(queries, keyvalue, doc_ids, owner_tiles, tile_counts):
    group_width = QUERY_HEADS // KEY_VALUE_HEADS
    row_block = min(512, SLAB_TOKENS)
    query_heads = queries.reshape(SLAB_TOKENS, KEY_VALUE_HEADS, group_width, HEAD_WIDTH)
    keyvalue_heads = keyvalue.reshape(SLAB_TOKENS, KEY_VALUE_HEADS, 2, HEAD_WIDTH)
    padded_extent = jnp.zeros((DOCUMENT_LIMIT, KEY_VALUE_HEADS, 2, HEAD_WIDTH), keyvalue.dtype)
    kv_pad = jnp.concatenate([padded_extent, keyvalue_heads], axis=0)
    docs_pad = jnp.concatenate([jnp.full((DOCUMENT_LIMIT,), -1, jnp.int32), doc_ids.astype(jnp.int32)], axis=0)

    def one_block(block_id):
        begin_row = block_id * row_block
        q_block = lax.dynamic_slice_in_dim(query_heads, begin_row, row_block, 0)
        kv_block = lax.dynamic_slice_in_dim(kv_pad, begin_row, row_block + DOCUMENT_LIMIT, 0)
        q_docs = lax.dynamic_slice_in_dim(doc_ids.astype(jnp.int32), begin_row, row_block, 0)
        k_docs = lax.dynamic_slice_in_dim(docs_pad, begin_row, row_block + DOCUMENT_LIMIT, 0)
        q_place = jnp.arange(row_block, dtype=jnp.int32) + DOCUMENT_LIMIT
        k_place = jnp.arange(row_block + DOCUMENT_LIMIT, dtype=jnp.int32)
        allowed = (q_docs[:, None] == k_docs[None, :]) & (k_place[None, :] <= q_place[:, None])
        result = attend(q_block, kv_block[:, :, 0], kv_block[:, :, 1], allowed)
        return result.reshape(row_block, QUERY_HEADS * HEAD_WIDTH)

    attended = lax.map(one_block, jnp.arange(SLAB_TOKENS // row_block, dtype=jnp.int32)).reshape(SLAB_TOKENS, QUERY_HEADS * HEAD_WIDTH)
    tiles = attended.reshape(NTILE, TILE, QUERY_HEADS * HEAD_WIDTH)
    picked = jnp.take(tiles, owner_tiles.reshape(-1).astype(jnp.int32), axis=0)
    live = (jnp.arange(CAP, dtype=jnp.int32)[None, :] < tile_counts[:, None]).reshape(-1)
    owned = jnp.where(live[:, None, None], picked, jnp.zeros((), attended.dtype))
    return owned.reshape(N_SEQ * CAP * TILE, QUERY_HEADS * HEAD_WIDTH)
```

```python
import functools
import math

import jax
import jax.numpy as jnp
from jax import lax
from jax.experimental import pallas as pl
from jax.experimental.pallas import tpu as pltpu
from jax.sharding import PartitionSpec as P

QUERY_HEADS = 64
KEY_VALUE_HEADS = 8
HEAD_WIDTH = 128
TILE = 128
DOCUMENT_LIMIT = 512

MESH = pl.DeviceIdType.MESH
NEAR_TILES = DOCUMENT_LIMIT // TILE + 1
BACK = NEAR_TILES - 1
GROUP_HEADS = QUERY_HEADS // KEY_VALUE_HEADS
HALF_HEADS = GROUP_HEADS // 2
HALF_COLS = HALF_HEADS * HEAD_WIDTH
PART_COLS = HALF_COLS // 2
GROUP_COLS = 2 * HALF_COLS
KV_COLS = 2 * HEAD_WIDTH
MASKED = -1e30
ROUNDS = 2
RAISE = HEAD_WIDTH ** -0.5 * math.log2(math.e)
VMEM = pl.BlockSpec(memory_space=pltpu.VMEM)
SMEM = pl.BlockSpec(memory_space=pltpu.SMEM)
HBM = pl.BlockSpec(memory_space=pltpu.HBM)
DMA = pltpu.SemaphoreType.DMA


class Place:
    def __init__(self, groups, count):
        self.me = me = lax.axis_index("seq")
        self.group = group = lax.axis_index("groups")
        self.core = lax.rem(me, 2)
        self.chip = chip = lax.div(me, 2)
        self.line = lax.rem(chip, 2)
        self.depth = lax.div(chip, 2)
        self.depths = count // 4
        self.reach = reach = self.depths // 2
        self.low = low = self.depth < reach
        step = jnp.where(low, 4, -4)
        self.inner = me + step
        self.outer = me - step
        self.rim = jnp.where(low, self.depth, self.depths - 1 - self.depth)
        self.crossing = self.rim == reach - 1
        self.sibling = me + 1 - 2 * self.core
        self.partner = lax.rem(me + count // 2, count)
        across = group + 1 - 2 * lax.rem(group, 2)
        beside = me + 2 - 4 * self.line
        self.giving = (jnp.where(low, across, group), jnp.where(low, me, beside))
        self.taking = (jnp.where(low, group, across), jnp.where(low, beside, me))


def remote(src, dst, send_sem, recv_sem, seq, group=None):
    to = {"seq": seq} if group is None else {"groups": group, "seq": seq}
    return pltpu.make_async_remote_copy(
        src_ref=src, dst_ref=dst, send_sem=send_sem, recv_sem=recv_sem,
        device_id=to, device_id_type=MESH)


class Flow:
    def __init__(self, at, rounds, o, sib, plan, far, farn, fars, farns, exo, exi, inj, injin, sends, recvs, turn):
        self.__dict__.update(locals())

    def trade(self, r, h):
        group, seq = self.at.giving
        return remote(self.exo.at[r, h], self.exi.at[r, h],
                      self.sends.at[0, r, h], self.recvs.at[0, r, h], seq, group)

    def inward(self, r, h):
        return remote(self.inj.at[r, h], self.injin.at[r, h],
                      self.sends.at[1, r, h], self.recvs.at[1, r, h], self.at.inner)

    def across(self, r, h):
        return remote(self.inj.at[r, h], self.far.at[r, h],
                      self.sends.at[1, r, h], self.recvs.at[2, r, h], self.at.inner)

    def outward(self, r, h):
        return remote(self.far.at[r, h], self.far.at[r, h],
                      self.sends.at[2, r, h], self.recvs.at[2, r, h], self.at.outer)

    def deliver(self, r, h):
        group, seq = self.at.taking
        return remote(self.far.at[r, h], self.farn.at[r, h],
                      self.sends.at[3, r, h], self.recvs.at[3, r, h], seq, group)

    def hand(self, r, h):
        return remote(self.far.at[r, h], self.fars.at[r, h],
                      self.sends.at[4, r, h], self.recvs.at[4, r, h], self.at.sibling)

    def handn(self, r, h):
        return remote(self.farn.at[r, h], self.farns.at[r, h],
                      self.sends.at[5, r, h], self.recvs.at[5, r, h], self.at.sibling)

    def here(self, row, r):
        return jnp.broadcast_to(self.plan[8 * row:8 * row + 1, :] == self.turn(r), (TILE, TILE))

    def offer(self, h):
        for r in range(self.rounds):
            own_here = self.here(0, r)
            for c in range(0, PART_COLS, TILE):
                cols, there = slice(c, c + TILE), slice(PART_COLS + c, PART_COLS + c + TILE)
                own = self.o[h, self.at.core, :, there].astype(jnp.float32)
                sib = self.sib[h, :, there].astype(jnp.float32)
                self.exo[r, h, :, cols] = jnp.where(own_here, own, sib).astype(jnp.bfloat16)
            self.trade(r, h).start()

    def compose(self, r, h, below):
        own_here, sib_here = self.here(0, r), self.here(1, r)
        nbr_here = self.here(2, r) | self.here(3, r)
        for c in range(0, PART_COLS, TILE):
            cols = slice(c, c + TILE)
            new = self.exi[r, h, :, cols].astype(jnp.float32)
            if below:
                new = jnp.where(nbr_here, new, self.injin[r, h, :, cols].astype(jnp.float32))
            new = jnp.where(sib_here, self.sib[h, :, cols].astype(jnp.float32), new)
            own = self.o[h, self.at.core, :, cols].astype(jnp.float32)
            self.inj[r, h, :, cols] = jnp.where(own_here, own, new).astype(jnp.bfloat16)

    def inject(self, h):
        for r in range(self.rounds):
            self.trade(r, h).wait_recv()

            @pl.when(self.at.rim == 0)
            def _():
                self.compose(r, h, False)

            @pl.when(self.at.rim > 0)
            def _():
                self.inward(r, h).wait_recv()
                self.compose(r, h, True)

            @pl.when(self.at.crossing)
            def _():
                self.across(r, h).start()

            @pl.when(jnp.logical_not(self.at.crossing))
            def _():
                self.inward(r, h).start()

    def forward(self, h):
        for r in range(self.rounds):
            self.outward(r, h).wait_recv()

            @pl.when(self.at.rim > 0)
            def _():
                self.outward(r, h).start()

            self.deliver(r, h).start()
            self.hand(r, h).start()

    def finish(self, h):
        for r in range(self.rounds):
            self.deliver(r, h).wait_recv()
            self.handn(r, h).start()

    def stages(self, first):
        at = self.at
        arrive = first + 1 + at.reach + at.reach - 1 - at.rim
        return ((first, self.offer), (first + 1 + at.rim, self.inject),
                (arrive, self.forward), (arrive + 1, self.finish))

    def steps(self, first):
        return KEY_VALUE_HEADS + first + 1 + 2 * self.at.reach

    def drain(self, h):
        for r in range(self.rounds):
            self.trade(r, h).wait_send()
            self.inward(r, h).wait_send()

            @pl.when(self.at.rim > 0)
            def _():
                self.outward(r, h).wait_send()

            self.deliver(r, h).wait_send()
            self.hand(r, h).wait()
            self.handn(r, h).wait()


def each(n, body):
    lax.fori_loop(0, n, lambda i, c: (body(i), c)[1], 0)


heads = functools.partial(each, KEY_VALUE_HEADS)


def run_stages(steps, stages):
    def step(u):
        for lag, stage in stages:
            h = u - lag

            @pl.when((h >= 0) & (h < KEY_VALUE_HEADS))
            def _():
                stage(h)

    each(steps, step)


def main_kernel(groups, count, kv_hbm, q_hbm, docs, counts,
                o, sib, far, farn, fars, farns, plan,
                q, kv, mark, marks, given, gathered, bias, vals, exo, exi, inj, injin,
                ql, kvl, share_s, share_r, mark_s, mark_r, given_s, given_r, info_s, info_r,
                kv_s, kv_r, flow_s, flow_r):
    at = Place(groups, count)
    me, core, chip, line, group = at.me, at.core, at.chip, at.line, at.group
    chips = count // 2
    flow = Flow(at, ROUNDS, o, sib, plan, far, farn, fars, farns, exo, exi, inj, injin,
                flow_s, flow_r, lambda r: r)

    def own(h):
        return kv_hbm.at[:, pl.ds(pl.multiple_of(h * KV_COLS, KV_COLS), KV_COLS)]

    def local(h):
        return pltpu.make_async_copy(own(h), kv.at[h, 4 + core], kvl.at[h])

    def q_copy(h):
        cols = pl.ds(pl.multiple_of(h * GROUP_COLS, GROUP_COLS), GROUP_COLS)
        return pltpu.make_async_copy(q_hbm.at[:, cols], q.at[:, cols], ql.at[h])

    def share(h):
        return remote(o.at[h, 1 - core], sib.at[h], share_s.at[h], share_r.at[h], at.sibling)

    def up_two(h):
        return remote(own(h), kv.at[h, core], kv_s.at[0, h], kv_r.at[h, core], me + 4)

    def up_one(h):
        return remote(own(h), kv.at[h, 2 + core], kv_s.at[1, h], kv_r.at[h, 2 + core], me + 2)

    def relay_one(h):
        return remote(kv.at[h, core], kv.at[h, 2 + core], kv_s.at[1, h], kv_r.at[h, 2 + core], me - 2)

    def sib_own(h):
        return remote(own(h), kv.at[h, 4], kv_s.at[2, h], kv_r.at[h, 4], at.sibling)

    def sib_one(h):
        return remote(kv.at[h, 2 + core], kv.at[h, 2 + core], kv_s.at[3, h],
                      kv_r.at[h, 2 + core], at.sibling)

    def sib_two(h):
        return remote(kv.at[h, 1], kv.at[h, 1], kv_s.at[4, h], kv_r.at[h, 1], at.sibling)

    def arrived(h, slot):
        remote(kv.at[h, slot], kv.at[h, slot], kv_s.at[0, h], kv_r.at[h, slot],
               at.sibling).wait_recv()

    def mark_to(k):
        return remote(mark, marks.at[BACK - k], mark_s.at[BACK - k], mark_r.at[BACK - k], me + k)

    def given_to(by):
        return remote(given.at[group], given.at[group], given_s.at[by], given_r.at[group],
                      me, lax.rem(group + by, groups))

    def given_from(by):
        other = lax.rem(group + by, groups)
        return remote(given.at[other], given.at[other], given_s.at[by], given_r.at[other], me, other)

    def info_to(peer):
        return remote(given, gathered.at[me], info_s.at[peer], info_r.at[me], peer)

    def info_from(peer):
        return remote(given, gathered.at[peer], info_s.at[peer], info_r.at[peer], peer)

    def peers(body):
        def one(i):
            body(lax.rem(me + 1 + i, count))
        each(count - 1, one)

    heads(lambda h: local(h).start())
    heads(lambda h: q_copy(h).start())
    mark[...] = jnp.broadcast_to(docs[...], (8, TILE))
    given[group] = jnp.full((8, TILE), counts[0], jnp.int32)

    barrier = pltpu.get_barrier_semaphore()
    peers(lambda p: pl.semaphore_signal(barrier, inc=1, device_id={"seq": p}, device_id_type=MESH))
    for by in range(1, groups):
        pl.semaphore_signal(barrier, inc=1, device_id={"groups": lax.rem(group + by, groups)},
                            device_id_type=MESH)
    pl.semaphore_wait(barrier, count - 1 + groups - 1)

    has_two_up = chip + 2 < chips

    def launch(h):
        @pl.when(has_two_up)
        def _():
            up_two(h).start()

        @pl.when(line == 0)
        def _():
            up_one(h).start()

        @pl.when(core == 0)
        def _():
            sib_own(h).start()

    launch(0)
    for by in range(1, groups):
        given_to(by).start()
    for k in range(1, NEAR_TILES):
        @pl.when(me + k < count)
        def _():
            mark_to(k).start()
    each(KEY_VALUE_HEADS - 1, lambda h: launch(h + 1))

    blank = jnp.zeros((TILE, KV_COLS), jnp.bfloat16)

    @pl.when(chip < 2)
    def _():
        def clear(h):
            kv[h, 0] = blank
            kv[h, 1] = blank
        heads(clear)

    @pl.when(chip < 1)
    def _():
        def clear(h):
            kv[h, 2] = blank
            kv[h, 3] = blank
        heads(clear)

    vals[:, HEAD_WIDTH:] = jnp.ones((NEAR_TILES * TILE, HEAD_WIDTH), jnp.bfloat16)

    for by in range(1, groups):
        given_from(by).wait_recv()
    peers(lambda p: info_to(p).start())
    gathered[me] = given[...]

    rows = lax.broadcasted_iota(jnp.int32, (TILE, TILE), 0)
    cols = lax.broadcasted_iota(jnp.int32, (TILE, TILE), 1)
    mine = jnp.broadcast_to(mark[0:1, :], (TILE, TILE))
    asked = mine.T
    bias[:, BACK * TILE:] = jnp.where((asked == mine) & (cols <= rows), 0.0, MASKED).astype(jnp.float32)
    for w in range(BACK):
        past = slice(w * TILE, (w + 1) * TILE)

        @pl.when(me - BACK + w < 0)
        def _():
            bias[:, past] = jnp.full((TILE, TILE), MASKED, jnp.float32)

        @pl.when(me - BACK + w >= 0)
        def _():
            mark_to(BACK - w).wait_recv()
            allowed = asked == jnp.broadcast_to(marks[w, 0:1, :], (TILE, TILE))
            bias[:, past] = jnp.where(allowed, 0.0, MASKED).astype(jnp.float32)

    def tally():
        peers(lambda p: info_from(p).wait_recv())
        half = count // 2
        other_group, other = at.giving
        other_sib = other + 1 - 2 * core
        targets = ((group, me), (group, at.sibling), (other_group, other), (other_group, other_sib),
                   (group, at.partner))

        def bin_of(g, i):
            up = i < half
            return jnp.where(up, 2 * lax.div(g, 2) + lax.rem(lax.div(i, 2), 2), groups + g)

        wanted = [(bin_of(g, i), g * count + i) for g, i in targets]

        def add(i, carry):
            ahead, totals = carry
            for g in range(groups):
                gives = jnp.where(gathered[i, g] == 0, 1, 0)
                here, order = bin_of(g, i), g * count + i
                ahead = tuple(
                    a + gives * jnp.where((here == b) & (order < n), 1, 0)
                    for a, (b, n) in zip(ahead, wanted))
                totals = tuple(t + gives * jnp.where(here == b, 1, 0) for b, t in enumerate(totals))
            return ahead, totals

        zero = jnp.zeros((8, TILE), jnp.int32)
        ahead, totals = lax.fori_loop(
            0, count, add, ((zero,) * len(targets), (zero,) * (2 * groups)))
        for slot, ((g, i), a) in enumerate(zip(targets, ahead)):
            gives = gathered[i, g] == 0
            plan[8 * slot:8 * slot + 8, :] = jnp.where(gives, a, -1)
        most = totals[0]
        for t in totals[1:]:
            most = jnp.maximum(most, t)
        plan[8 * len(targets):8 * len(targets) + 8, :] = most

    def attend(h):
        vals[:, 0:HEAD_WIDTH] = kv[h, pl.ds(core, NEAR_TILES), :, HEAD_WIDTH:].reshape(
            NEAR_TILES * TILE, HEAD_WIDTH)
        keys = kv[h, pl.ds(core, NEAR_TILES), :, 0:HEAD_WIDTH].reshape(NEAR_TILES * TILE, HEAD_WIDTH)
        summed = vals[...]
        for j in range(GROUP_HEADS):
            at_col = pl.multiple_of((h * GROUP_HEADS + j) * HEAD_WIDTH, HEAD_WIDTH)
            s = lax.dot_general(q[:, pl.ds(at_col, HEAD_WIDTH)], keys, (((1,), (1,)), ((), ())),
                                preferred_element_type=jnp.float32) + bias[...]
            e = jnp.exp2((s - jnp.max(s, axis=1, keepdims=True)) * RAISE)
            mixed = jnp.dot(e.astype(jnp.bfloat16), summed, preferred_element_type=jnp.float32)
            c = (j % HALF_HEADS) * HEAD_WIDTH
            o[h, j // HALF_HEADS, :, c:c + HEAD_WIDTH] = (
                mixed[:, 0:HEAD_WIDTH] / mixed[:, HEAD_WIDTH:]).astype(jnp.bfloat16)

    def relay_two(h):
        @pl.when(chip >= 2)
        def _():
            arrived(h, core)

            @pl.when(line == 1)
            def _():
                relay_one(h).start()

            @pl.when(core == 1)
            def _():
                sib_two(h).start()

    def relay_sib(h):
        @pl.when(chip >= 1)
        def _():
            arrived(h, 2 + core)
            sib_one(h).start()

    def compute(h):
        @pl.when(chip >= 1)
        def _():
            arrived(h, 3 - core)

        @pl.when((chip >= 2) & (core == 0))
        def _():
            arrived(h, 1)

        @pl.when(core == 1)
        def _():
            arrived(h, 4)

        local(h).wait()
        q_copy(h).wait()
        attend(h)
        share(h).start()

    def shared(h):
        @pl.when(h == 0)
        def _():
            tally()

        share(h).wait_recv()

    stages = ((0, relay_two), (1, relay_sib), (2, compute), (3, shared)) + flow.stages(3)
    run_stages(flow.steps(3), stages)

    def drain(h):
        flow.drain(h)
        share(h).wait_send()

        @pl.when(has_two_up)
        def _():
            up_two(h).wait_send()

        @pl.when((line == 0) | (chip >= 2))
        def _():
            up_one(h).wait_send()

        @pl.when(core == 0)
        def _():
            sib_own(h).wait_send()

        @pl.when(chip >= 1)
        def _():
            sib_one(h).wait_send()

        @pl.when((chip >= 2) & (core == 1))
        def _():
            sib_two(h).wait_send()

    heads(drain)
    peers(lambda p: info_to(p).wait_send())
    for by in range(1, groups):
        given_to(by).wait_send()
    for k in range(1, NEAR_TILES):
        @pl.when(me + k < count)
        def _():
            mark_to(k).wait_send()


def round_kernel(groups, count, o, sib, plan, turn, far, farn, fars, farns,
                 exo, exi, inj, injin, flow_s, flow_r):
    at = Place(groups, count)
    barrier = pltpu.get_barrier_semaphore()

    def greet(seq, group=at.group):
        pl.semaphore_signal(barrier, inc=1, device_id={"groups": group, "seq": seq}, device_id_type=MESH)

    greet(at.sibling)
    greet(at.inner)
    greet(at.giving[1], at.giving[0])
    greet(at.taking[1], at.taking[0])

    @pl.when(at.rim > 0)
    def _():
        greet(at.outer)

    pl.semaphore_wait(barrier, jnp.where(at.rim > 0, 5, 4))

    flow = Flow(at, 1, o, sib, plan, far, farn, fars, farns, exo, exi, inj, injin,
                flow_s, flow_r, lambda r: turn[0:1, :])
    run_stages(flow.steps(0), flow.stages(0))
    heads(flow.drain)


def place_kernel(extra, tiles, valid, plan, o, *rest):
    fars, out, blank, sems = rest[:-3], rest[-3], rest[-2], rest[-1]
    me = lax.axis_index("seq")
    core = lax.rem(me, 2)
    slots = out.shape[0] // TILE
    blank[...] = jnp.zeros_like(blank)
    rank = plan[4 * 8, 0]
    main, late = fars[:4], fars[4:]
    turn = jnp.clip(rank, 0, ROUNDS - 1)

    def spot(h, lane, part):
        at = (2 * h + lane) * HALF_COLS + part * PART_COLS
        return pl.ds(pl.multiple_of(at, PART_COLS), PART_COLS)

    def parts(h):
        mine = [(o.at[h, lane, :, pl.ds(part * PART_COLS, PART_COLS)], spot(h, lane, part))
                for lane in (0, 1) for part in (0, 1)]
        where = [spot(h, lane, part) for lane in (core, 1 - core) for part in (0, 1)]
        theirs = [(ref.at[turn, h], cols) for ref, cols in zip(main, where)]
        later = [(ref.at[0, h], cols) for ref, cols in zip(late, where)]
        none = [(blank, cols) for _, cols in mine]
        return mine, theirs, later, none

    def run(h, c, go):
        for s in range(slots):
            live = s < valid[0]
            own = live & (tiles[0, s] == me)
            moved = live & jnp.logical_not(own)
            soon = moved & (rank < ROUNDS) if extra else moved
            cases = (own, soon, moved & (rank >= ROUNDS), jnp.logical_not(live))
            for case, pieces in zip(cases, parts(h)):
                if not pieces:
                    continue

                @pl.when(case)
                def _():
                    for k, (src, cols) in enumerate(pieces):
                        go(pltpu.make_async_copy(
                            src, out.at[pl.ds(s * TILE, TILE), cols], sems.at[h, s, k]))
        return c

    lax.fori_loop(0, KEY_VALUE_HEADS, functools.partial(run, go=lambda x: x.start()), 0)
    lax.fori_loop(0, KEY_VALUE_HEADS, functools.partial(run, go=lambda x: x.wait()), 0)


def local(groups, count, queries, keyvalue, doc_ids, owner_tiles, tile_counts):
    width = queries.shape[1]
    slots = owner_tiles.shape[1]
    H = KEY_VALUE_HEADS
    bf, i32 = jnp.bfloat16, jnp.int32
    half = (H, TILE, HALF_COLS)

    def part(rounds):
        return (rounds, H, TILE, PART_COLS)

    *held, plan = pl.pallas_call(
        functools.partial(main_kernel, groups, count),
        out_shape=[
            jax.ShapeDtypeStruct((H, 2, TILE, HALF_COLS), bf),
            jax.ShapeDtypeStruct(half, bf),
        ] + [jax.ShapeDtypeStruct(part(ROUNDS), bf)] * 4 + [
            jax.ShapeDtypeStruct((48, TILE), i32),
        ],
        in_specs=[HBM, HBM, VMEM, SMEM],
        out_specs=[VMEM] * 7,
        scratch_shapes=[
            pltpu.VMEM(queries.shape, bf),
            pltpu.VMEM((H, 6, TILE, KV_COLS), bf),
            pltpu.VMEM((8, TILE), i32),
            pltpu.VMEM((BACK, 8, TILE), i32),
            pltpu.VMEM((groups, 8, TILE), i32),
            pltpu.VMEM((count, groups, 8, TILE), i32),
            pltpu.VMEM((TILE, NEAR_TILES * TILE), jnp.float32),
            pltpu.VMEM((NEAR_TILES * TILE, 2 * HEAD_WIDTH), bf),
        ] + [pltpu.VMEM(part(ROUNDS), bf)] * 4 + [
            DMA((H,)),
            DMA((H,)),
            DMA((H,)),
            DMA((H,)),
            DMA((BACK,)),
            DMA((BACK,)),
            DMA((groups,)),
            DMA((groups,)),
            DMA((count,)),
            DMA((count,)),
            DMA((5, H)),
            DMA((H, 6)),
            DMA((6, ROUNDS, H)),
            DMA((6, ROUNDS, H)),
        ],
        compiler_params=pltpu.CompilerParams(
            collective_id=0, has_side_effects=True, vmem_limit_bytes=40 << 20),
    )(keyvalue, queries, doc_ids[None, :], tile_counts)
    o, sib, *far = held

    def again(turn):
        turns = jnp.full((8, TILE), turn, i32)
        return pl.pallas_call(
            functools.partial(round_kernel, groups, count),
            out_shape=[jax.ShapeDtypeStruct(part(1), bf)] * 4,
            in_specs=[VMEM] * 4,
            out_specs=[VMEM] * 4,
            scratch_shapes=[pltpu.VMEM(part(1), bf)] * 4 + [DMA((6, 1, H)), DMA((6, 1, H))],
            compiler_params=pltpu.CompilerParams(
                collective_id=1, has_side_effects=True, vmem_limit_bytes=24 << 20),
        )(o, sib, plan, turns)

    def place(late):
        return pl.pallas_call(
            functools.partial(place_kernel, bool(late)),
            out_shape=jax.ShapeDtypeStruct((slots * TILE, width), bf),
            in_specs=[SMEM] * 3 + [VMEM] * (5 + len(late)),
            out_specs=pl.BlockSpec(memory_space=pl.ANY),
            scratch_shapes=[pltpu.VMEM((TILE, PART_COLS), bf), DMA((H, slots, 4))],
            compiler_params=pltpu.CompilerParams(vmem_limit_bytes=16 << 20),
        )(owner_tiles, tile_counts, plan, o, *far, *late)

    most = plan[40, 0]

    def more():
        def one(turn, kept):
            here = plan[32, 0] == turn
            return tuple(jnp.where(here, n, k) for n, k in zip(again(turn), kept))

        return place(lax.fori_loop(ROUNDS, most, one, tuple(jnp.zeros(part(1), bf) for _ in range(4))))

    return lax.cond(most > ROUNDS, more, lambda: place(()))


def solution(mesh):
    spread = P(("groups", "seq"))
    rows = P(("groups", "seq"), None)
    return jax.shard_map(
        functools.partial(local, mesh.shape["groups"], mesh.shape["seq"]), mesh=mesh,
        in_specs=(rows, rows, spread, rows, spread), out_specs=rows, check_vma=False)
```

```python
import functools
import math

import jax
import jax.numpy as jnp
from jax import lax
from jax.experimental import pallas as pl
from jax.experimental.pallas import tpu as pltpu
from jax.sharding import PartitionSpec as P

QUERY_HEADS = 64
KEY_VALUE_HEADS = 8
HEAD_WIDTH = 128
TILE = 128
DOCUMENT_LIMIT = 512

MESH = pl.DeviceIdType.MESH
NEAR_TILES = DOCUMENT_LIMIT // TILE + 1
BACK = NEAR_TILES - 1
GROUP_HEADS = QUERY_HEADS // KEY_VALUE_HEADS
HALF_HEADS = GROUP_HEADS // 2
HALF_COLS = HALF_HEADS * HEAD_WIDTH
PART_COLS = HALF_COLS // 2
GROUP_COLS = 2 * HALF_COLS
KV_COLS = 2 * HEAD_WIDTH
MASKED = -1e30
SPLITS = 1
HOP = 3
FUSED = 4
RAISE = HEAD_WIDTH ** -0.5 * math.log2(math.e)
VMEM = pl.BlockSpec(memory_space=pltpu.VMEM)
SMEM = pl.BlockSpec(memory_space=pltpu.SMEM)
HBM = pl.BlockSpec(memory_space=pltpu.HBM)
DMA = pltpu.SemaphoreType.DMA


class Place:
    def __init__(self, groups, count):
        self.me = me = lax.axis_index("seq")
        self.group = group = lax.axis_index("groups")
        self.core = lax.rem(me, 2)
        self.chip = chip = lax.div(me, 2)
        self.line = lax.rem(chip, 2)
        self.depth = lax.div(chip, 2)
        self.depths = count // 4
        self.reach = reach = self.depths // 2
        self.low = low = self.depth < reach
        step = jnp.where(low, 4, -4)
        self.inner = me + step
        self.outer = me - step
        self.rim = jnp.where(low, self.depth, self.depths - 1 - self.depth)
        self.crossing = self.rim == reach - 1
        self.sibling = me + 1 - 2 * self.core
        self.partner = lax.rem(me + count // 2, count)
        across = group + 1 - 2 * lax.rem(group, 2)
        beside = me + 2 - 4 * self.line
        self.giving = (jnp.where(low, across, group), jnp.where(low, me, beside))
        self.taking = (jnp.where(low, group, across), jnp.where(low, beside, me))


def remote(src, dst, send_sem, recv_sem, seq, group=None):
    to = {"seq": seq} if group is None else {"groups": group, "seq": seq}
    return pltpu.make_async_remote_copy(
        src_ref=src, dst_ref=dst, send_sem=send_sem, recv_sem=recv_sem,
        device_id=to, device_id_type=MESH)


class Flow:
    def __init__(self, at, rounds, splits, o, sib, plan, far, farn, fars, farns, exo, exi, inj, injin,
                 sends, recvs, turn):
        self.__dict__.update(locals())
        self.items = KEY_VALUE_HEADS * splits * rounds
        self.rows = TILE // splits

    def copy(self, kind, i, src, dst, seq, group=None, lands=None):
        lands = kind if lands is None else lands
        return remote(src.at[i], dst.at[i], self.sends.at[kind, i], self.recvs.at[lands, i], seq, group)

    def trade(self, i):
        group, seq = self.at.giving
        return self.copy(0, i, self.exo, self.exi, seq, group)

    def inward(self, i):
        return self.copy(1, i, self.inj, self.injin, self.at.inner)

    def across(self, i):
        return self.copy(1, i, self.inj, self.far, self.at.inner, lands=2)

    def outward(self, i):
        return self.copy(2, i, self.far, self.far, self.at.outer)

    def deliver(self, i):
        group, seq = self.at.taking
        return self.copy(3, i, self.far, self.farn, seq, group)

    def hand(self, i):
        return self.copy(4, i, self.far, self.fars, self.at.sibling)

    def handn(self, i):
        return self.copy(5, i, self.farn, self.farns, self.at.sibling)

    def spot(self, i):
        h = lax.div(i, self.splits * self.rounds)
        p = lax.rem(lax.div(i, self.rounds), self.splits)
        rows = pl.ds(pl.multiple_of(p * self.rows, self.rows), self.rows)
        turn = self.turn(lax.rem(i, self.rounds))
        heres = [jnp.broadcast_to(self.plan[8 * k:8 * k + 1, :] == turn, (self.rows, TILE)) for k in range(4)]
        return h, rows, heres

    def offer(self, i):
        h, rows, (own_here, *_) = self.spot(i)
        for c in range(0, PART_COLS, TILE):
            cols, there = slice(c, c + TILE), slice(PART_COLS + c, PART_COLS + c + TILE)
            own = self.o[h, self.at.core, rows, there].astype(jnp.float32)
            sib = self.sib[h, rows, there].astype(jnp.float32)
            self.exo[i, :, cols] = jnp.where(own_here, own, sib).astype(jnp.bfloat16)
        self.trade(i).start()

    def compose(self, i, below):
        h, rows, (own_here, sib_here, near, far) = self.spot(i)
        nbr_here = near | far
        for c in range(0, PART_COLS, TILE):
            cols = slice(c, c + TILE)
            new = self.exi[i, :, cols].astype(jnp.float32)
            if below:
                new = jnp.where(nbr_here, new, self.injin[i, :, cols].astype(jnp.float32))
            new = jnp.where(sib_here, self.sib[h, rows, cols].astype(jnp.float32), new)
            own = self.o[h, self.at.core, rows, cols].astype(jnp.float32)
            self.inj[i, :, cols] = jnp.where(own_here, own, new).astype(jnp.bfloat16)

    def inject(self, i):
        self.trade(i).wait_recv()

        @pl.when(self.at.rim == 0)
        def _():
            self.compose(i, False)

        @pl.when(self.at.rim > 0)
        def _():
            self.inward(i).wait_recv()
            self.compose(i, True)

        @pl.when(self.at.crossing)
        def _():
            self.across(i).start()

        @pl.when(jnp.logical_not(self.at.crossing))
        def _():
            self.inward(i).start()

    def forward(self, i):
        self.outward(i).wait_recv()

        @pl.when(self.at.rim > 0)
        def _():
            self.outward(i).start()

        self.deliver(i).start()
        self.hand(i).start()

    def finish(self, i):
        self.deliver(i).wait_recv()
        self.handn(i).start()

    def stages(self, first, hop):
        at = self.at
        arrive = first + hop * (2 * at.reach - at.rim)
        return ((arrive + hop, 1, self.items, self.finish), (arrive, 1, self.items, self.forward),
                (first + hop * (1 + at.rim), 1, self.items, self.inject), (first, 1, self.items, self.offer))

    def steps(self, first, hop):
        return self.items + first + hop * (2 * self.at.reach + 1)

    def drain(self, i):
        self.trade(i).wait_send()
        self.inward(i).wait_send()

        @pl.when(self.at.rim > 0)
        def _():
            self.outward(i).wait_send()

        self.deliver(i).wait_send()
        self.hand(i).wait()
        self.handn(i).wait()


def each(n, body):
    lax.fori_loop(0, n, lambda i, c: (body(i), c)[1], 0)


heads = functools.partial(each, KEY_VALUE_HEADS)


def run_stages(steps, stages):
    def step(u):
        for lag, pace, count, stage in stages:
            v = u - lag
            due = (v >= 0) & (v < count * pace)
            if pace > 1:
                due = due & (lax.rem(v, pace) == 0)

            @pl.when(due)
            def _():
                stage(lax.div(v, pace) if pace > 1 else v)

    each(steps, step)


def main_kernel(groups, count, kv_hbm, q_hbm, docs_hbm, counts,
                o, sib, plan,
                q, kv, docs_in, mark, marks, given, gathered, bias, vals,
                ql, kvl, docs_s, share_s, share_r, mark_s, mark_r, given_s, given_r, info_s, info_r,
                kv_s, kv_r):
    at = Place(groups, count)
    me, core, chip, line, group = at.me, at.core, at.chip, at.line, at.group
    chips = count // 2
    def own(h):
        return kv_hbm.at[:, pl.ds(pl.multiple_of(h * KV_COLS, KV_COLS), KV_COLS)]

    def local(h):
        return pltpu.make_async_copy(own(h), kv.at[h, 4 + core], kvl.at[h])

    def q_copy(h):
        cols = pl.ds(pl.multiple_of(h * GROUP_COLS, GROUP_COLS), GROUP_COLS)
        return pltpu.make_async_copy(q_hbm.at[:, cols], q.at[:, cols], ql.at[h])

    def share(h):
        return remote(o.at[h, 1 - core], sib.at[h], share_s.at[h], share_r.at[h], at.sibling)

    def up_two(h):
        return remote(own(h), kv.at[h, core], kv_s.at[0, h], kv_r.at[h, core], me + 4)

    def up_one(h):
        return remote(own(h), kv.at[h, 2 + core], kv_s.at[1, h], kv_r.at[h, 2 + core], me + 2)

    def relay_one(h):
        return remote(kv.at[h, core], kv.at[h, 2 + core], kv_s.at[1, h], kv_r.at[h, 2 + core], me - 2)

    def sib_own(h):
        return remote(own(h), kv.at[h, 4], kv_s.at[2, h], kv_r.at[h, 4], at.sibling)

    def sib_one(h):
        return remote(kv.at[h, 2 + core], kv.at[h, 2 + core], kv_s.at[3, h],
                      kv_r.at[h, 2 + core], at.sibling)

    def sib_two(h):
        return remote(kv.at[h, 1], kv.at[h, 1], kv_s.at[4, h], kv_r.at[h, 1], at.sibling)

    def arrived(h, slot):
        remote(kv.at[h, slot], kv.at[h, slot], kv_s.at[0, h], kv_r.at[h, slot],
               at.sibling).wait_recv()

    def mark_to(k):
        return remote(mark, marks.at[BACK - k], mark_s.at[BACK - k], mark_r.at[BACK - k], me + k)

    def given_to(by):
        return remote(given.at[group], given.at[group], given_s.at[by], given_r.at[group],
                      me, lax.rem(group + by, groups))

    def given_from(by):
        other = lax.rem(group + by, groups)
        return remote(given.at[other], given.at[other], given_s.at[by], given_r.at[other], me, other)

    def info_to(peer):
        return remote(given, gathered.at[me], info_s.at[peer], info_r.at[me], peer)

    def info_from(peer):
        return remote(given, gathered.at[peer], info_s.at[peer], info_r.at[peer], peer)

    def peers(body):
        def one(i):
            body(lax.rem(me + 1 + i, count))
        each(count - 1, one)

    docs = pltpu.make_async_copy(docs_hbm, docs_in, docs_s)
    docs.start()
    heads(lambda h: local(h).start())
    heads(lambda h: q_copy(h).start())
    given[group] = jnp.full((8, TILE), counts[0], jnp.int32)

    barrier = pltpu.get_barrier_semaphore()
    peers(lambda p: pl.semaphore_signal(barrier, inc=1, device_id={"seq": p}, device_id_type=MESH))
    for by in range(1, groups):
        pl.semaphore_signal(barrier, inc=1, device_id={"groups": lax.rem(group + by, groups)},
                            device_id_type=MESH)
    docs.wait()
    mark[...] = jnp.broadcast_to(docs_in[...], (8, TILE))
    pl.semaphore_wait(barrier, count - 1 + groups - 1)

    has_two_up = chip + 2 < chips

    def launch(h):
        @pl.when(has_two_up)
        def _():
            up_two(h).start()

        @pl.when(line == 0)
        def _():
            up_one(h).start()

        @pl.when(core == 0)
        def _():
            sib_own(h).start()

    launch(0)
    for by in range(1, groups):
        given_to(by).start()
    for k in range(1, NEAR_TILES):
        @pl.when(me + k < count)
        def _():
            mark_to(k).start()
    each(KEY_VALUE_HEADS - 1, lambda h: launch(h + 1))

    blank = jnp.zeros((TILE, KV_COLS), jnp.bfloat16)

    @pl.when(chip < 2)
    def _():
        def clear(h):
            kv[h, 0] = blank
            kv[h, 1] = blank
        heads(clear)

    @pl.when(chip < 1)
    def _():
        def clear(h):
            kv[h, 2] = blank
            kv[h, 3] = blank
        heads(clear)

    vals[:, HEAD_WIDTH:] = jnp.ones((NEAR_TILES * TILE, HEAD_WIDTH), jnp.bfloat16)

    for by in range(1, groups):
        given_from(by).wait_recv()
    peers(lambda p: info_to(p).start())
    gathered[me] = given[...]

    rows = lax.broadcasted_iota(jnp.int32, (TILE, TILE), 0)
    cols = lax.broadcasted_iota(jnp.int32, (TILE, TILE), 1)
    mine = jnp.broadcast_to(mark[0:1, :], (TILE, TILE))
    asked = mine.T
    bias[:, BACK * TILE:] = jnp.where((asked == mine) & (cols <= rows), 0.0, MASKED).astype(jnp.float32)
    for w in range(BACK):
        past = slice(w * TILE, (w + 1) * TILE)

        @pl.when(me - BACK + w < 0)
        def _():
            bias[:, past] = jnp.full((TILE, TILE), MASKED, jnp.float32)

        @pl.when(me - BACK + w >= 0)
        def _():
            mark_to(BACK - w).wait_recv()
            allowed = asked == jnp.broadcast_to(marks[w, 0:1, :], (TILE, TILE))
            bias[:, past] = jnp.where(allowed, 0.0, MASKED).astype(jnp.float32)

    def tally():
        peers(lambda p: info_from(p).wait_recv())
        half = count // 2
        other_group, other = at.giving
        other_sib = other + 1 - 2 * core
        targets = ((group, me), (group, at.sibling), (other_group, other), (other_group, other_sib),
                   (group, at.partner))

        def bin_of(g, i):
            up = i < half
            return jnp.where(up, 2 * lax.div(g, 2) + lax.rem(lax.div(i, 2), 2), groups + g)

        wanted = [(bin_of(g, i), g * count + i) for g, i in targets]

        def add(i, carry):
            ahead, totals = carry
            for g in range(groups):
                gives = jnp.where(gathered[i, g] == 0, 1, 0)
                here, order = bin_of(g, i), g * count + i
                ahead = tuple(
                    a + gives * jnp.where((here == b) & (order < n), 1, 0)
                    for a, (b, n) in zip(ahead, wanted))
                totals = tuple(t + gives * jnp.where(here == b, 1, 0) for b, t in enumerate(totals))
            return ahead, totals

        zero = jnp.zeros((8, TILE), jnp.int32)
        ahead, totals = lax.fori_loop(
            0, count, add, ((zero,) * len(targets), (zero,) * (2 * groups)))
        for slot, ((g, i), a) in enumerate(zip(targets, ahead)):
            gives = gathered[i, g] == 0
            plan[8 * slot:8 * slot + 8, :] = jnp.where(gives, a, -1)
        most = totals[0]
        for t in totals[1:]:
            most = jnp.maximum(most, t)
        plan[8 * len(targets):8 * len(targets) + 8, :] = most

    def attend(h):
        vals[:, 0:HEAD_WIDTH] = kv[h, pl.ds(core, NEAR_TILES), :, HEAD_WIDTH:].reshape(
            NEAR_TILES * TILE, HEAD_WIDTH)
        keys = kv[h, pl.ds(core, NEAR_TILES), :, 0:HEAD_WIDTH].reshape(NEAR_TILES * TILE, HEAD_WIDTH)
        summed = vals[...]
        for j in range(GROUP_HEADS):
            at_col = pl.multiple_of((h * GROUP_HEADS + j) * HEAD_WIDTH, HEAD_WIDTH)
            s = lax.dot_general(q[:, pl.ds(at_col, HEAD_WIDTH)], keys, (((1,), (1,)), ((), ())),
                                preferred_element_type=jnp.float32) + bias[...]
            e = jnp.exp2((s - jnp.max(s, axis=1, keepdims=True)) * RAISE)
            mixed = jnp.dot(e.astype(jnp.bfloat16), summed, preferred_element_type=jnp.float32)
            c = (j % HALF_HEADS) * HEAD_WIDTH
            o[h, j // HALF_HEADS, :, c:c + HEAD_WIDTH] = (
                mixed[:, 0:HEAD_WIDTH] / mixed[:, HEAD_WIDTH:]).astype(jnp.bfloat16)

    def relay_two(h):
        @pl.when(chip >= 2)
        def _():
            arrived(h, core)

            @pl.when(line == 1)
            def _():
                relay_one(h).start()

            @pl.when(core == 1)
            def _():
                sib_two(h).start()

    def relay_sib(h):
        @pl.when(chip >= 1)
        def _():
            arrived(h, 2 + core)
            sib_one(h).start()

    def compute(h):
        @pl.when(chip >= 1)
        def _():
            arrived(h, 3 - core)

        @pl.when((chip >= 2) & (core == 0))
        def _():
            arrived(h, 1)

        @pl.when(core == 1)
        def _():
            arrived(h, 4)

        local(h).wait()
        q_copy(h).wait()
        attend(h)
        share(h).start()

    run_stages(KEY_VALUE_HEADS + 3, tuple((lag, 1, KEY_VALUE_HEADS, stage) for lag, stage in (
        (0, relay_two), (2, relay_sib), (3, compute))))
    tally()

    def drain(h):
        share(h).wait()

        @pl.when(has_two_up)
        def _():
            up_two(h).wait_send()

        @pl.when((line == 0) | (chip >= 2))
        def _():
            up_one(h).wait_send()

        @pl.when(core == 0)
        def _():
            sib_own(h).wait_send()

        @pl.when(chip >= 1)
        def _():
            sib_one(h).wait_send()

        @pl.when((chip >= 2) & (core == 1))
        def _():
            sib_two(h).wait_send()

    heads(drain)
    peers(lambda p: info_to(p).wait_send())
    for by in range(1, groups):
        given_to(by).wait_send()
    for k in range(1, NEAR_TILES):
        @pl.when(me + k < count)
        def _():
            mark_to(k).wait_send()


def round_kernel(groups, count, rounds, o, sib, plan, turn, far, farn, fars, farns,
                 exo, exi, inj, injin, flow_s, flow_r):
    at = Place(groups, count)
    barrier = pltpu.get_barrier_semaphore()

    def greet(seq, group=at.group):
        pl.semaphore_signal(barrier, inc=1, device_id={"groups": group, "seq": seq}, device_id_type=MESH)

    greet(at.sibling)
    greet(at.inner)
    greet(at.giving[1], at.giving[0])
    greet(at.taking[1], at.taking[0])

    @pl.when(at.rim > 0)
    def _():
        greet(at.outer)

    pl.semaphore_wait(barrier, jnp.where(at.rim > 0, 5, 4))

    flow = Flow(at, rounds, SPLITS, o, sib, plan, far, farn, fars, farns, exo, exi, inj, injin,
                flow_s, flow_r, lambda r: turn[0:1, :] + r)
    run_stages(flow.steps(0, HOP), flow.stages(0, HOP))
    each(flow.items, flow.drain)


def place_kernel(rounds, tiles, valid, plan, o, far, farn, fars, farns, out, blank, sems):
    me = lax.axis_index("seq")
    core = lax.rem(me, 2)
    slots = out.shape[0] // TILE
    blank[...] = jnp.zeros_like(blank)
    turn = jnp.clip(plan[4 * 8, 0], 0, rounds - 1)

    def spot(h, lane, part=0, width=PART_COLS):
        at = (2 * h + lane) * HALF_COLS + part * PART_COLS
        return pl.ds(pl.multiple_of(at, width), width)

    def parts(h):
        mine = [(o.at[h, lane], 0, TILE, spot(h, lane, 0, HALF_COLS)) for lane in (0, 1)]
        where = [spot(h, lane, part) for lane in (core, 1 - core) for part in (0, 1)]
        theirs = [(ref.at[(h * SPLITS + p) * rounds + turn], p * (TILE // SPLITS), TILE // SPLITS, cols)
                  for ref, cols in zip((far, farn, fars, farns), where) for p in range(SPLITS)]
        none = [(blank, 0, TILE, pl.ds(pl.multiple_of(h * GROUP_COLS, GROUP_COLS), GROUP_COLS))]
        return mine, theirs, none

    def run(h, c, go):
        for s in range(slots):
            live = s < valid[0]
            own = live & (tiles[0, s] == me)
            cases = (own, live & jnp.logical_not(own), jnp.logical_not(live))
            for case, pieces in zip(cases, parts(h)):
                @pl.when(case)
                def _():
                    for k, (src, row, rows, cols) in enumerate(pieces):
                        go(pltpu.make_async_copy(
                            src, out.at[pl.ds(s * TILE + row, rows), cols], sems.at[h, s, k]))
        return c

    lax.fori_loop(0, KEY_VALUE_HEADS, functools.partial(run, go=lambda x: x.start()), 0)
    lax.fori_loop(0, KEY_VALUE_HEADS, functools.partial(run, go=lambda x: x.wait()), 0)


def local(groups, count, queries, keyvalue, doc_ids, owner_tiles, tile_counts):
    width = queries.shape[1]
    slots = owner_tiles.shape[1]
    H = KEY_VALUE_HEADS
    bf, i32 = jnp.bfloat16, jnp.int32

    def stay(x):
        return pltpu.with_memory_space_constraint(x, pltpu.HBM)

    def near(x):
        return pltpu.with_memory_space_constraint(x, pltpu.VMEM)

    o, sib, plan = pl.pallas_call(
        functools.partial(main_kernel, groups, count),
        out_shape=[
            pltpu.VMEM((H, 2, TILE, HALF_COLS), bf),
            pltpu.VMEM((H, TILE, HALF_COLS), bf),
            pltpu.VMEM((48, TILE), i32),
        ],
        in_specs=[HBM, HBM, HBM, SMEM],
        out_specs=[VMEM] * 3,
        scratch_shapes=[
            pltpu.VMEM(queries.shape, bf),
            pltpu.VMEM((H, 6, TILE, KV_COLS), bf),
            pltpu.VMEM((1, TILE), i32),
            pltpu.VMEM((8, TILE), i32),
            pltpu.VMEM((BACK, 8, TILE), i32),
            pltpu.VMEM((groups, 8, TILE), i32),
            pltpu.VMEM((count, groups, 8, TILE), i32),
            pltpu.VMEM((TILE, NEAR_TILES * TILE), jnp.float32),
            pltpu.VMEM((NEAR_TILES * TILE, 2 * HEAD_WIDTH), bf),
            DMA((H,)),
            DMA((H,)),
            DMA(()),
            DMA((H,)),
            DMA((H,)),
            DMA((BACK,)),
            DMA((BACK,)),
            DMA((groups,)),
            DMA((groups,)),
            DMA((count,)),
            DMA((count,)),
            DMA((5, H)),
            DMA((H, 6)),
        ],
        compiler_params=pltpu.CompilerParams(
            collective_id=0, has_side_effects=True, vmem_limit_bytes=16 << 20),
    )(stay(keyvalue), stay(queries), stay(doc_ids[None, :]), tile_counts)

    def rounds_from(turn, rounds, number):
        items = H * SPLITS * rounds
        part = pltpu.VMEM((items, TILE // SPLITS, PART_COLS), bf)
        return pl.pallas_call(
            functools.partial(round_kernel, groups, count, rounds),
            out_shape=[part] * 4,
            in_specs=[VMEM] * 4,
            out_specs=[VMEM] * 4,
            scratch_shapes=[part] * 4 + [DMA((6, items))] * 2,
            compiler_params=pltpu.CompilerParams(
                collective_id=number, has_side_effects=True, vmem_limit_bytes=(8 + 4 * rounds) << 20),
        )(near(o), near(sib), near(plan), jnp.full((8, TILE), turn, i32))

    def place(rounds, far):
        return pl.pallas_call(
            functools.partial(place_kernel, rounds),
            out_shape=pltpu.HBM((slots * TILE, width), bf),
            in_specs=[SMEM] * 3 + [VMEM] * 5,
            out_specs=pl.BlockSpec(memory_space=pl.ANY),
            scratch_shapes=[pltpu.VMEM((TILE, GROUP_COLS), bf), DMA((H, slots, 4 * SPLITS))],
            compiler_params=pltpu.CompilerParams(vmem_limit_bytes=8 << 20),
        )(owner_tiles, tile_counts, plan, near(o), *map(near, far))

    most = plan[40, 0]

    def fused(rounds):
        return lambda: place(rounds, rounds_from(0, rounds, rounds))

    def one_by_one():
        def again(turn, kept):
            here = plan[32, 0] == turn
            return tuple(jnp.where(here, n, k) for n, k in zip(rounds_from(turn, 1, FUSED + 1), kept))

        empty = jnp.zeros((H * SPLITS, TILE // SPLITS, PART_COLS), bf)
        return place(1, lax.fori_loop(0, most, again, (empty,) * 4))

    return lax.switch(jnp.minimum(most, FUSED + 1) - 1,
                      [fused(r) for r in range(1, FUSED + 1)] + [one_by_one])


def solution(mesh):
    spread = P(("groups", "seq"))
    rows = P(("groups", "seq"), None)
    return jax.shard_map(
        functools.partial(local, mesh.shape["groups"], mesh.shape["seq"]), mesh=mesh,
        in_specs=(rows, rows, spread, rows, spread), out_specs=rows, check_vma=False)
```

```python
import functools
import math

import jax
import jax.numpy as jnp
from jax import lax
from jax.experimental import pallas as pl
from jax.experimental.pallas import tpu as pltpu
from jax.sharding import PartitionSpec as P

QUERY_HEADS = 64
KEY_VALUE_HEADS = 8
HEAD_WIDTH = 128
TILE = 128
DOCUMENT_LIMIT = 512

MESH = pl.DeviceIdType.MESH
NEAR_TILES = DOCUMENT_LIMIT // TILE + 1
BACK = NEAR_TILES - 1
GROUP_HEADS = QUERY_HEADS // KEY_VALUE_HEADS
HALF_HEADS = GROUP_HEADS // 2
HALF_COLS = HALF_HEADS * HEAD_WIDTH
PART_COLS = HALF_COLS // 2
GROUP_COLS = 2 * HALF_COLS
KV_COLS = 2 * HEAD_WIDTH
MASKED = -1e30
SPLITS = 1
HOP = 3
FUSED = 4
SEATS = 5
PLAN = 8 * (SEATS + 1)
RAISE = HEAD_WIDTH ** -0.5 * math.log2(math.e)
VMEM = pl.BlockSpec(memory_space=pltpu.VMEM)
SMEM = pl.BlockSpec(memory_space=pltpu.SMEM)
HBM = pl.BlockSpec(memory_space=pltpu.HBM)
DMA = pltpu.SemaphoreType.DMA


class Place:
    def __init__(self, groups, count, swap=False):
        self.me = me = lax.axis_index("seq")
        self.group = group = lax.axis_index("groups")
        self.core = lax.rem(me, 2)
        self.chip = chip = lax.div(me, 2)
        self.line = lax.rem(chip, 2)
        self.depth = lax.div(chip, 2)
        self.depths = count // 4
        self.reach = reach = self.depths // 2
        self.low = low = self.depth < reach
        step = jnp.where(low, 4, -4)
        self.inner = me + step
        self.outer = me - step
        self.rim = jnp.where(low, self.depth, self.depths - 1 - self.depth)
        self.crossing = self.rim == reach - 1
        self.sibling = me + 1 - 2 * self.core
        self.partner = lax.rem(me + count // 2, count)
        across = group + 1 - 2 * lax.rem(group, 2)
        beside = me + 2 - 4 * self.line
        first, second = jnp.where(low, across, group), jnp.where(low, me, beside)
        third, fourth = jnp.where(low, group, across), jnp.where(low, beside, me)
        self.giving, self.taking = (first, second), (third, fourth)
        if swap:
            self.giving, self.taking = self.taking, self.giving


def remote(src, dst, send_sem, recv_sem, seq, group=None):
    to = {"seq": seq} if group is None else {"groups": group, "seq": seq}
    return pltpu.make_async_remote_copy(
        src_ref=src, dst_ref=dst, send_sem=send_sem, recv_sem=recv_sem,
        device_id=to, device_id_type=MESH)


class Flow:
    def __init__(self, at, rounds, splits, base, o, sib, plan, far, farn, fars, farns, exo, exi, inj, injin,
                 sends, recvs, turn):
        self.__dict__.update(locals())
        self.items = KEY_VALUE_HEADS * splits * rounds
        self.rows = TILE // splits

    def copy(self, kind, i, src, dst, seq, group=None, lands=None):
        lands = kind if lands is None else lands
        return remote(src.at[i], dst.at[i], self.sends.at[kind, i], self.recvs.at[lands, i], seq, group)

    def trade(self, i):
        group, seq = self.at.giving
        return self.copy(0, i, self.exo, self.exi, seq, group)

    def inward(self, i):
        return self.copy(1, i, self.inj, self.injin, self.at.inner)

    def across(self, i):
        return self.copy(1, i, self.inj, self.far, self.at.inner, lands=2)

    def outward(self, i):
        return self.copy(2, i, self.far, self.far, self.at.outer)

    def deliver(self, i):
        group, seq = self.at.taking
        return self.copy(3, i, self.far, self.farn, seq, group)

    def hand(self, i):
        return self.copy(4, i, self.far, self.fars, self.at.sibling)

    def handn(self, i):
        return self.copy(5, i, self.farn, self.farns, self.at.sibling)

    def spot(self, i):
        h = lax.div(i, self.splits * self.rounds)
        p = lax.rem(lax.div(i, self.rounds), self.splits)
        rows = pl.ds(pl.multiple_of(p * self.rows, self.rows), self.rows)
        turn = self.turn(lax.rem(i, self.rounds))
        heres = [jnp.broadcast_to(self.plan[self.base + 8 * k:self.base + 8 * k + 1, :] == turn, (self.rows, TILE)) for k in range(4)]
        return h, rows, heres

    def offer(self, i):
        h, rows, (own_here, *_) = self.spot(i)
        for c in range(0, PART_COLS, TILE):
            cols, there = slice(c, c + TILE), slice(PART_COLS + c, PART_COLS + c + TILE)
            own = self.o[h, self.at.core, rows, there].astype(jnp.float32)
            sib = self.sib[h, rows, there].astype(jnp.float32)
            self.exo[i, :, cols] = jnp.where(own_here, own, sib).astype(jnp.bfloat16)
        self.trade(i).start()

    def compose(self, i, below):
        h, rows, (own_here, sib_here, near, far) = self.spot(i)
        nbr_here = near | far
        for c in range(0, PART_COLS, TILE):
            cols = slice(c, c + TILE)
            new = self.exi[i, :, cols].astype(jnp.float32)
            if below:
                new = jnp.where(nbr_here, new, self.injin[i, :, cols].astype(jnp.float32))
            new = jnp.where(sib_here, self.sib[h, rows, cols].astype(jnp.float32), new)
            own = self.o[h, self.at.core, rows, cols].astype(jnp.float32)
            self.inj[i, :, cols] = jnp.where(own_here, own, new).astype(jnp.bfloat16)

    def inject(self, i):
        self.trade(i).wait_recv()

        @pl.when(self.at.rim == 0)
        def _():
            self.compose(i, False)

        @pl.when(self.at.rim > 0)
        def _():
            self.inward(i).wait_recv()
            self.compose(i, True)

        @pl.when(self.at.crossing)
        def _():
            self.across(i).start()

        @pl.when(jnp.logical_not(self.at.crossing))
        def _():
            self.inward(i).start()

    def forward(self, i):
        self.outward(i).wait_recv()

        @pl.when(self.at.rim > 0)
        def _():
            self.outward(i).start()

        self.deliver(i).start()
        self.hand(i).start()

    def finish(self, i):
        self.deliver(i).wait_recv()
        self.handn(i).start()

    def stages(self, first, hop):
        at = self.at
        arrive = first + hop * (2 * at.reach - at.rim)
        return ((arrive + hop, 1, self.items, self.finish), (arrive, 1, self.items, self.forward),
                (first + hop * (1 + at.rim), 1, self.items, self.inject), (first, 1, self.items, self.offer))

    def steps(self, first, hop):
        return self.items + first + hop * (2 * self.at.reach + 1)

    def drain(self, i):
        self.trade(i).wait_send()
        self.inward(i).wait_send()

        @pl.when(self.at.rim > 0)
        def _():
            self.outward(i).wait_send()

        self.deliver(i).wait_send()
        self.hand(i).wait()
        self.handn(i).wait()


def each(n, body):
    lax.fori_loop(0, n, lambda i, c: (body(i), c)[1], 0)


heads = functools.partial(each, KEY_VALUE_HEADS)


def run_stages(steps, stages):
    def step(u):
        for lag, pace, count, stage in stages:
            v = u - lag
            due = (v >= 0) & (v < count * pace)
            if pace > 1:
                due = due & (lax.rem(v, pace) == 0)

            @pl.when(due)
            def _():
                stage(lax.div(v, pace) if pace > 1 else v)

    each(steps, step)


def main_kernel(groups, count, kv_hbm, q_hbm, docs_hbm, counts,
                o, sib, plan,
                q, kv, docs_in, mark, marks, given, gathered, bias, vals,
                ql, kvl, docs_s, share_s, share_r, mark_s, mark_r, given_s, given_r, info_s, info_r,
                kv_s, kv_r):
    at = Place(groups, count)
    me, core, chip, line, group = at.me, at.core, at.chip, at.line, at.group
    chips = count // 2
    def own(h):
        return kv_hbm.at[:, pl.ds(pl.multiple_of(h * KV_COLS, KV_COLS), KV_COLS)]

    def local(h):
        return pltpu.make_async_copy(own(h), kv.at[h, 4 + core], kvl.at[h])

    def q_copy(h):
        cols = pl.ds(pl.multiple_of(h * GROUP_COLS, GROUP_COLS), GROUP_COLS)
        return pltpu.make_async_copy(q_hbm.at[:, cols], q.at[:, cols], ql.at[h])

    def share(h):
        return remote(o.at[h, 1 - core], sib.at[h], share_s.at[h], share_r.at[h], at.sibling)

    def up_two(h):
        return remote(own(h), kv.at[h, core], kv_s.at[0, h], kv_r.at[h, core], me + 4)

    def up_one(h):
        return remote(own(h), kv.at[h, 2 + core], kv_s.at[1, h], kv_r.at[h, 2 + core], me + 2)

    def relay_one(h):
        return remote(kv.at[h, core], kv.at[h, 2 + core], kv_s.at[1, h], kv_r.at[h, 2 + core], me - 2)

    def sib_own(h):
        return remote(own(h), kv.at[h, 4], kv_s.at[2, h], kv_r.at[h, 4], at.sibling)

    def sib_one(h):
        return remote(kv.at[h, 2 + core], kv.at[h, 2 + core], kv_s.at[3, h],
                      kv_r.at[h, 2 + core], at.sibling)

    def sib_two(h):
        return remote(kv.at[h, 1], kv.at[h, 1], kv_s.at[4, h], kv_r.at[h, 1], at.sibling)

    def arrived(h, slot):
        remote(kv.at[h, slot], kv.at[h, slot], kv_s.at[0, h], kv_r.at[h, slot],
               at.sibling).wait_recv()

    def mark_to(k):
        return remote(mark, marks.at[BACK - k], mark_s.at[BACK - k], mark_r.at[BACK - k], me + k)

    def given_to(by):
        return remote(given.at[group], given.at[group], given_s.at[by], given_r.at[group],
                      me, lax.rem(group + by, groups))

    def given_from(by):
        other = lax.rem(group + by, groups)
        return remote(given.at[other], given.at[other], given_s.at[by], given_r.at[other], me, other)

    def info_to(peer):
        return remote(given, gathered.at[me], info_s.at[peer], info_r.at[me], peer)

    def info_from(peer):
        return remote(given, gathered.at[peer], info_s.at[peer], info_r.at[peer], peer)

    def peers(body):
        def one(i):
            body(lax.rem(me + 1 + i, count))
        each(count - 1, one)

    docs = pltpu.make_async_copy(docs_hbm, docs_in, docs_s)
    docs.start()
    heads(lambda h: local(h).start())
    heads(lambda h: q_copy(h).start())
    given[group] = jnp.full((8, TILE), counts[0], jnp.int32)

    barrier = pltpu.get_barrier_semaphore()
    peers(lambda p: pl.semaphore_signal(barrier, inc=1, device_id={"seq": p}, device_id_type=MESH))
    for by in range(1, groups):
        pl.semaphore_signal(barrier, inc=1, device_id={"groups": lax.rem(group + by, groups)},
                            device_id_type=MESH)
    docs.wait()
    mark[...] = jnp.broadcast_to(docs_in[...], (8, TILE))
    pl.semaphore_wait(barrier, count - 1 + groups - 1)

    has_two_up = chip + 2 < chips

    def launch(h):
        @pl.when(has_two_up)
        def _():
            up_two(h).start()

        @pl.when(line == 0)
        def _():
            up_one(h).start()

        @pl.when(core == 0)
        def _():
            sib_own(h).start()

    launch(0)
    for by in range(1, groups):
        given_to(by).start()
    for k in range(1, NEAR_TILES):
        @pl.when(me + k < count)
        def _():
            mark_to(k).start()
    each(KEY_VALUE_HEADS - 1, lambda h: launch(h + 1))

    blank = jnp.zeros((TILE, KV_COLS), jnp.bfloat16)

    @pl.when(chip < 2)
    def _():
        def clear(h):
            kv[h, 0] = blank
            kv[h, 1] = blank
        heads(clear)

    @pl.when(chip < 1)
    def _():
        def clear(h):
            kv[h, 2] = blank
            kv[h, 3] = blank
        heads(clear)

    vals[:, HEAD_WIDTH:] = jnp.ones((NEAR_TILES * TILE, HEAD_WIDTH), jnp.bfloat16)

    for by in range(1, groups):
        given_from(by).wait_recv()
    peers(lambda p: info_to(p).start())
    gathered[me] = given[...]

    rows = lax.broadcasted_iota(jnp.int32, (TILE, TILE), 0)
    cols = lax.broadcasted_iota(jnp.int32, (TILE, TILE), 1)
    mine = jnp.broadcast_to(mark[0:1, :], (TILE, TILE))
    asked = mine.T
    bias[:, BACK * TILE:] = jnp.where((asked == mine) & (cols <= rows), 0.0, MASKED).astype(jnp.float32)
    for w in range(BACK):
        past = slice(w * TILE, (w + 1) * TILE)

        @pl.when(me - BACK + w < 0)
        def _():
            bias[:, past] = jnp.full((TILE, TILE), MASKED, jnp.float32)

        @pl.when(me - BACK + w >= 0)
        def _():
            mark_to(BACK - w).wait_recv()
            allowed = asked == jnp.broadcast_to(marks[w, 0:1, :], (TILE, TILE))
            bias[:, past] = jnp.where(allowed, 0.0, MASKED).astype(jnp.float32)

    def tally():
        peers(lambda p: info_from(p).wait_recv())
        half = count // 2
        lane = lax.broadcasted_iota(jnp.int32, (8, TILE), 1)

        def targets(swap):
            other_group, other = Place(groups, count, swap).giving
            return ((group, me), (group, at.sibling), (other_group, other),
                    (other_group, other + 1 - 2 * core), (group, at.partner))

        def bin_of(swap, g, i):
            pair, one = 2 * lax.div(g, 2) + lax.rem(lax.div(i, 2), 2), groups + g
            return jnp.where(i < half, one, pair) if swap else jnp.where(i < half, pair, one)

        def add(i, gives):
            return tuple(
                jnp.where((lane == i) & (gathered[i, g] == 0), 1.0, x) for g, x in enumerate(gives))

        gives = lax.fori_loop(0, count, add, (jnp.zeros((8, TILE), jnp.float32),) * groups)
        odd = (lane >> 1) & 1

        def amount(chosen):
            kept = [jnp.where(c, x, 0.0) for c, x in zip(chosen, gives)]
            whole = functools.reduce(lambda p, q: p + q, kept)
            return jnp.broadcast_to(jnp.sum(whole, axis=1, keepdims=True), (8, TILE)).astype(jnp.int32)

        mosts = []
        for swap in (False, True):
            bins = []
            for g in range(groups):
                pair, one = 2 * (g // 2) + odd, jnp.full((8, TILE), groups + g, jnp.int32)
                bins.append(jnp.where(lane < half, one, pair) if swap else jnp.where(lane < half, pair, one))
            for slot, (g, i) in enumerate(targets(swap)):
                b, n = bin_of(swap, g, i), g * count + i
                ahead = amount([(x == b) & (k * count + lane < n) for k, x in enumerate(bins)])
                row = swap * PLAN + 8 * slot
                plan[row:row + 8, :] = jnp.where(gathered[i, g] == 0, ahead, -1)
            most = functools.reduce(jnp.maximum, [amount([x == b for x in bins]) for b in range(2 * groups)])
            plan[swap * PLAN + 8 * SEATS:(swap + 1) * PLAN, :] = most
            mosts.append(most)
        straight, swapped = mosts
        least = jnp.minimum(straight, swapped)
        choice = jnp.where(straight <= swapped, straight - 1, FUSED + swapped - 1)
        plan[2 * PLAN:2 * PLAN + 8, :] = jnp.where(least > FUSED, 2 * FUSED, choice)

    def attend(h):
        vals[:, 0:HEAD_WIDTH] = kv[h, pl.ds(core, NEAR_TILES), :, HEAD_WIDTH:].reshape(
            NEAR_TILES * TILE, HEAD_WIDTH)
        keys = kv[h, pl.ds(core, NEAR_TILES), :, 0:HEAD_WIDTH].reshape(NEAR_TILES * TILE, HEAD_WIDTH)
        summed = vals[...]
        for j in range(GROUP_HEADS):
            at_col = pl.multiple_of((h * GROUP_HEADS + j) * HEAD_WIDTH, HEAD_WIDTH)
            s = lax.dot_general(q[:, pl.ds(at_col, HEAD_WIDTH)], keys, (((1,), (1,)), ((), ())),
                                preferred_element_type=jnp.float32) + bias[...]
            e = jnp.exp2((s - jnp.max(s, axis=1, keepdims=True)) * RAISE)
            mixed = jnp.dot(e.astype(jnp.bfloat16), summed, preferred_element_type=jnp.float32)
            c = (j % HALF_HEADS) * HEAD_WIDTH
            o[h, j // HALF_HEADS, :, c:c + HEAD_WIDTH] = (
                mixed[:, 0:HEAD_WIDTH] / mixed[:, HEAD_WIDTH:]).astype(jnp.bfloat16)

    def relay_two(h):
        @pl.when(chip >= 2)
        def _():
            arrived(h, core)

            @pl.when(line == 1)
            def _():
                relay_one(h).start()

            @pl.when(core == 1)
            def _():
                sib_two(h).start()

    def relay_sib(h):
        @pl.when(chip >= 1)
        def _():
            arrived(h, 2 + core)
            sib_one(h).start()

    def compute(h):
        @pl.when(chip >= 1)
        def _():
            arrived(h, 3 - core)

        @pl.when((chip >= 2) & (core == 0))
        def _():
            arrived(h, 1)

        @pl.when(core == 1)
        def _():
            arrived(h, 4)

        local(h).wait()
        q_copy(h).wait()

        @pl.when(h == KEY_VALUE_HEADS // 2)
        def _():
            tally()

        attend(h)
        share(h).start()

    run_stages(KEY_VALUE_HEADS + 3, tuple((lag, 1, KEY_VALUE_HEADS, stage) for lag, stage in (
        (0, relay_two), (2, relay_sib), (3, compute))))

    def drain(h):
        share(h).wait()

        @pl.when(has_two_up)
        def _():
            up_two(h).wait_send()

        @pl.when((line == 0) | (chip >= 2))
        def _():
            up_one(h).wait_send()

        @pl.when(core == 0)
        def _():
            sib_own(h).wait_send()

        @pl.when(chip >= 1)
        def _():
            sib_one(h).wait_send()

        @pl.when((chip >= 2) & (core == 1))
        def _():
            sib_two(h).wait_send()

    heads(drain)
    peers(lambda p: info_to(p).wait_send())
    for by in range(1, groups):
        given_to(by).wait_send()
    for k in range(1, NEAR_TILES):
        @pl.when(me + k < count)
        def _():
            mark_to(k).wait_send()


def round_kernel(groups, count, rounds, swap, o, sib, plan, turn, far, farn, fars, farns,
                 exo, exi, inj, injin, flow_s, flow_r):
    at = Place(groups, count, swap)
    barrier = pltpu.get_barrier_semaphore()

    def greet(seq, group=at.group):
        pl.semaphore_signal(barrier, inc=1, device_id={"groups": group, "seq": seq}, device_id_type=MESH)

    greet(at.sibling)
    greet(at.inner)
    greet(at.giving[1], at.giving[0])
    greet(at.taking[1], at.taking[0])

    @pl.when(at.rim > 0)
    def _():
        greet(at.outer)

    pl.semaphore_wait(barrier, jnp.where(at.rim > 0, 5, 4))

    flow = Flow(at, rounds, SPLITS, PLAN if swap else 0, o, sib, plan, far, farn, fars, farns, exo, exi, inj, injin,
                flow_s, flow_r, lambda r: turn[0:1, :] + r)
    run_stages(flow.steps(0, HOP), flow.stages(0, HOP))
    each(flow.items, flow.drain)


def place_kernel(rounds, swap, tiles, valid, plan, o, far, farn, fars, farns, out, blank, sems):
    me = lax.axis_index("seq")
    core = lax.rem(me, 2)
    slots = out.shape[0] // TILE
    blank[...] = jnp.zeros_like(blank)
    row = (PLAN if swap else 0) + 8 * (SEATS - 1)
    turn = jnp.clip(jnp.max(plan[row:row + 8, :]), 0, rounds - 1)

    def spot(h, lane, part=0, width=PART_COLS):
        at = (2 * h + lane) * HALF_COLS + part * PART_COLS
        return pl.ds(pl.multiple_of(at, width), width)

    def parts(h):
        mine = [(o.at[h, lane], 0, TILE, spot(h, lane, 0, HALF_COLS)) for lane in (0, 1)]
        where = [spot(h, lane, part) for lane in (core, 1 - core) for part in (0, 1)]
        theirs = [(ref.at[(h * SPLITS + p) * rounds + turn], p * (TILE // SPLITS), TILE // SPLITS, cols)
                  for ref, cols in zip((far, farn, fars, farns), where) for p in range(SPLITS)]
        none = [(blank, 0, TILE, pl.ds(pl.multiple_of(h * GROUP_COLS, GROUP_COLS), GROUP_COLS))]
        return mine, theirs, none

    def run(h, c, go):
        for s in range(slots):
            live = s < valid[0]
            own = live & (tiles[0, s] == me)
            cases = (own, live & jnp.logical_not(own), jnp.logical_not(live))
            for case, pieces in zip(cases, parts(h)):
                @pl.when(case)
                def _():
                    for k, (src, row, rows, cols) in enumerate(pieces):
                        go(pltpu.make_async_copy(
                            src, out.at[pl.ds(s * TILE + row, rows), cols], sems.at[h, s, k]))
        return c

    lax.fori_loop(0, KEY_VALUE_HEADS, functools.partial(run, go=lambda x: x.start()), 0)
    lax.fori_loop(0, KEY_VALUE_HEADS, functools.partial(run, go=lambda x: x.wait()), 0)


def local(groups, count, queries, keyvalue, doc_ids, owner_tiles, tile_counts):
    width = queries.shape[1]
    slots = owner_tiles.shape[1]
    H = KEY_VALUE_HEADS
    bf, i32 = jnp.bfloat16, jnp.int32

    def stay(x):
        return pltpu.with_memory_space_constraint(x, pltpu.HBM)

    def near(x):
        return pltpu.with_memory_space_constraint(x, pltpu.VMEM)

    o, sib, plan = pl.pallas_call(
        functools.partial(main_kernel, groups, count),
        out_shape=[
            pltpu.VMEM((H, 2, TILE, HALF_COLS), bf),
            pltpu.VMEM((H, TILE, HALF_COLS), bf),
            pltpu.VMEM((2 * PLAN + 8, TILE), i32),
        ],
        in_specs=[HBM, HBM, HBM, SMEM],
        out_specs=[VMEM] * 3,
        scratch_shapes=[
            pltpu.VMEM(queries.shape, bf),
            pltpu.VMEM((H, 6, TILE, KV_COLS), bf),
            pltpu.VMEM((1, TILE), i32),
            pltpu.VMEM((8, TILE), i32),
            pltpu.VMEM((BACK, 8, TILE), i32),
            pltpu.VMEM((groups, 8, TILE), i32),
            pltpu.VMEM((count, groups, 8, TILE), i32),
            pltpu.VMEM((TILE, NEAR_TILES * TILE), jnp.float32),
            pltpu.VMEM((NEAR_TILES * TILE, 2 * HEAD_WIDTH), bf),
            DMA((H,)),
            DMA((H,)),
            DMA(()),
            DMA((H,)),
            DMA((H,)),
            DMA((BACK,)),
            DMA((BACK,)),
            DMA((groups,)),
            DMA((groups,)),
            DMA((count,)),
            DMA((count,)),
            DMA((5, H)),
            DMA((H, 6)),
        ],
        compiler_params=pltpu.CompilerParams(
            collective_id=0, has_side_effects=True, vmem_limit_bytes=16 << 20),
    )(stay(keyvalue), stay(queries), stay(doc_ids[None, :]), tile_counts)

    def rounds_from(turn, rounds, swap, number):
        items = H * SPLITS * rounds
        part = pltpu.VMEM((items, TILE // SPLITS, PART_COLS), bf)
        return pl.pallas_call(
            functools.partial(round_kernel, groups, count, rounds, swap),
            out_shape=[part] * 4,
            in_specs=[VMEM] * 4,
            out_specs=[VMEM] * 4,
            scratch_shapes=[part] * 4 + [DMA((6, items))] * 2,
            compiler_params=pltpu.CompilerParams(
                collective_id=number, has_side_effects=True, vmem_limit_bytes=(8 + 4 * rounds) << 20),
        )(near(o), near(sib), near(plan), jnp.full((8, TILE), turn, i32))

    def place(rounds, swap, far):
        return pl.pallas_call(
            functools.partial(place_kernel, rounds, swap),
            out_shape=pltpu.HBM((slots * TILE, width), bf),
            in_specs=[SMEM] * 2 + [VMEM] * 6,
            out_specs=pl.BlockSpec(memory_space=pl.ANY),
            scratch_shapes=[pltpu.VMEM((TILE, GROUP_COLS), bf), DMA((H, slots, 4 * SPLITS))],
            compiler_params=pltpu.CompilerParams(vmem_limit_bytes=8 << 20),
        )(owner_tiles, tile_counts, near(plan), near(o), *map(near, far))

    def fused(rounds, swap):
        return lambda: place(rounds, swap, rounds_from(0, rounds, swap, 1 + rounds + FUSED * swap))

    def one_by_one():
        def again(turn, kept):
            here = plan[8 * (SEATS - 1), 0] == turn
            return tuple(jnp.where(here, n, k) for n, k in zip(rounds_from(turn, 1, 0, 1), kept))

        empty = jnp.zeros((H * SPLITS, TILE // SPLITS, PART_COLS), bf)
        return place(1, 0, lax.fori_loop(0, plan[8 * SEATS, 0], again, (empty,) * 4))

    return lax.switch(
        plan[2 * PLAN, 0],
        [fused(r, swap) for swap in (0, 1) for r in range(1, FUSED + 1)] + [one_by_one])


def solution(mesh):
    spread = P(("groups", "seq"))
    rows = P(("groups", "seq"), None)
    return jax.shard_map(
        functools.partial(local, mesh.shape["groups"], mesh.shape["seq"]), mesh=mesh,
        in_specs=(rows, rows, spread, rows, spread), out_specs=rows, check_vma=False)
```
